32 devices in a mesh: mem: 4 (over y, x), strip: 8 (over z, core).
Axes of the slice: x: 2, y: 2, z: 4, core: 2. Of those that a mesh axis runs over, the one named last changes fastest.
Arguments:
- ensemble: float32 [256, 64, 256], P('mem', 'strip'), may hold values from -12 to 12
- forcing: float32 [64, 256], P('strip'), may hold values from 4 to 12
- obs_index: int32 [64, 128], P(('strip', 'mem')), may hold values from 0 to 255
- obs_count: int32 [64], P(('strip', 'mem')), may hold values from 1 to 128, as said below
- obs_value: float32 [64, 128], P(('strip', 'mem')), may hold values from -18 to 18
- obs_precision: float32 [64, 128], P(('strip', 'mem')), may hold values from 0.05 to 1
Outputs:
- analysis: float32 [256, 64, 256], P('mem', 'strip')
The draws below stay inside these ranges and needn't reach their ends.
Inputs may be any that keep to these rules, and one draw needn't show every extreme that they name: The live observations of a region are the first obs_count of its slots; in every draw some region has all 128 slots live. `obs_index`: position of the observed cell within its region; a cell may be observed more than once.
All inputs are finite; a program needn't handle non-finite values.
Results may differ from the reference program's by a relative error of at most 0.0003.
Values sent between devices are 32-bit elements; how exact they have to be, the bound alone decides.
A program may use at most 64 MiB of HBM per device.

```python
import math
import jax
import jax.numpy as jnp
from jax import lax

MEMBER_TOTAL = 256
STEPS = 4
NS_ITERS = 4
REGION_VALUES = 256
OBS_MAX = 128
NLAT = 64
LON = 256
REGION_TOTAL = 64


def draw_obs_count(key, part):
    key_counts, key_chosen = jax.random.split(jax.random.fold_in(key, 11))
    counts = jax.random.randint(key_counts, (REGION_TOTAL,), 1, OBS_MAX + 1, dtype=jnp.int32)
    chosen = jax.random.randint(key_chosen, (), 0, REGION_TOTAL, dtype=jnp.int32)
    return jnp.where(jnp.arange(REGION_TOTAL, dtype=jnp.int32) == chosen, jnp.int32(OBS_MAX), counts)


def place_ends(values, key, smallest, high):
    extent = values.shape
    place = [jax.random.randint(jax.random.fold_in(key, axis), (), 0, extent[axis]) for axis in range(len(extent))]
    values = values.at[tuple(place)].set(smallest)
    longest = extent.index(max(extent))
    place[longest] = (place[longest] + 1) % extent[longest]
    return values.at[tuple(place)].set(high)


def level_of(own_key, dims, pieces, smallest, high):
    gain, own = 1.0, jax.random.fold_in(own_key, 6)
    for axis_at, parts in pieces:
        heights = jnp.exp(jax.random.uniform(jax.random.fold_in(own, axis_at), (parts,), jnp.float32, smallest / len(pieces), high / len(pieces)))
        gain = gain * jnp.repeat(heights, dims[axis_at] // parts).reshape([-1 if axis == axis_at else 1 for axis in range(len(dims))])
    return gain


def noise(key, extent, deviation, most, pieces=(), held_as=jnp.bfloat16):
    gain = level_of(key, extent, pieces, -0.22, 0.18) if pieces else 1.0
    values = jax.random.normal(key, extent, jnp.float32) * deviation * gain
    return jnp.minimum(jnp.maximum(values, -most), most).astype(held_as)


def setup_inputs(seed: int = 0) -> dict:
    keys = jax.random.split(jax.random.key(seed), 7)
    return {
        "ensemble": noise(keys[0], (MEMBER_TOTAL, NLAT, LON), 2.0, 12.0, ((0, 4), (1, 8)), jnp.float32),
        "forcing": jnp.clip(4.0 + 8.0 * jax.random.uniform(keys[1], (NLAT, LON), jnp.float32) ** level_of(keys[1], (NLAT, LON), ((0, 8),), -0.2, 0.2), 4.0, 12.0),
        "obs_index": place_ends(jax.random.randint(keys[2], (REGION_TOTAL, OBS_MAX), 0, REGION_VALUES), jax.random.fold_in(keys[2], 1), 0, REGION_VALUES - 1).astype(jnp.int32),
        "obs_count": draw_obs_count(jax.random.fold_in(keys[6], 71), 0),
        "obs_value": noise(keys[4], (REGION_TOTAL, OBS_MAX), 3.0, 18.0, ((0, 32),), jnp.float32),
        "obs_precision": jnp.clip(jnp.exp(math.log(1.0) - 2.9957323 * jax.random.uniform(keys[5], (REGION_TOTAL, OBS_MAX), jnp.float32) ** level_of(keys[5], (REGION_TOTAL, OBS_MAX), ((0, 32),), -0.2, 0.2)), 0.05, 1.0),
    }


step_size = 0.05
coupling = 0.4

def predict_increment(present_state, forcing):
    zero_row = jnp.zeros((1, present_state.shape[1]), present_state.dtype)
    padded_state = jnp.concatenate([zero_row, present_state, zero_row], axis=0)
    meridional = padded_state[2:] + padded_state[:-2] - 2.0 * present_state
    advection = (jnp.roll(present_state, -1, 1) - jnp.roll(present_state, 2, 1)) * jnp.roll(present_state, 1, 1)
    return present_state + step_size * (advection - present_state + forcing) + coupling * meridional

def analyze(members, obs_index, obs_count, obs_value, obs_precision):
    highest = lax.Precision.HIGHEST
    ens_size = members.shape[0]
    member_mean = lax.optimization_barrier(jnp.mean(members, axis=0))
    spread = members - member_mean[None]
    cell_ids = jnp.arange(members.shape[2], dtype=jnp.int32)
    onehot = (obs_index[:, :, None] == cell_ids[None, None, :]).astype(jnp.float32)
    slot_ids = jnp.arange(obs_index.shape[1], dtype=jnp.int32)
    live_mask = (slot_ids[None, :] < obs_count[:, None]).astype(jnp.float32)
    obs_spread = jnp.einsum('roc,krc->rok', onehot, spread, precision=highest)
    obs_mean = jnp.einsum('roc,rc->ro', onehot, member_mean, precision=highest)
    weight = obs_precision * live_mask
    innovation = weight * (obs_value - obs_mean)
    gram_matrix = jnp.einsum('roj,rok->rjk', obs_spread * weight[:, :, None], obs_spread, precision=highest)
    identity = jnp.eye(ens_size, dtype=jnp.float32)
    norm_scale = ens_size - 1.0 + jnp.sqrt(lax.optimization_barrier(jnp.sum(gram_matrix * gram_matrix, axis=(1, 2))))
    left_iterate = ((ens_size - 1.0) * identity + gram_matrix) / norm_scale[:, None, None]
    right_iterate = jnp.broadcast_to(identity, gram_matrix.shape)
    for repeat in range(NS_ITERS):
        correction = 1.5 * identity - 0.5 * jnp.einsum('rij,rjk->rik', right_iterate, left_iterate, precision=highest)
        left_iterate = jnp.einsum('rij,rjk->rik', left_iterate, correction, precision=highest)
        right_iterate = jnp.einsum('rij,rjk->rik', correction, right_iterate, precision=highest)
    inv_root = right_iterate / jnp.sqrt(norm_scale)[:, None, None]
    projected = jnp.einsum('roj,ro->rj', obs_spread, innovation, precision=highest)
    halfway = jnp.einsum('rjk,rk->rj', inv_root, projected, precision=highest)
    mean_weights = jnp.einsum('rjk,rk->rj', inv_root, halfway, precision=highest)
    transform = math.sqrt(ens_size - 1.0) * inv_root + mean_weights[:, :, None]
    return member_mean[None] + jnp.einsum('rjk,jrc->krc', transform, spread, precision=highest)

def reference(ensemble, forcing, obs_index, obs_count, obs_value, obs_precision):

    def integrate_model(member_state):
        for repeat in range(STEPS):
            member_state = predict_increment(member_state, forcing)
        return member_state
    predicted_state = lax.map(integrate_model, ensemble)
    region_blocks = predicted_state.reshape(MEMBER_TOTAL, REGION_TOTAL, REGION_VALUES).transpose(1, 0, 2)

    def solve_region(packed):
        members, index_row, count_one, value_row, precision_row = packed
        result = analyze(members[:, None, :], index_row[None], count_one[None], value_row[None], precision_row[None])
        return result[:, 0, :]
    analysis = lax.map(solve_region, (region_blocks, obs_index, obs_count, obs_value, obs_precision))
    return analysis.transpose(1, 0, 2).reshape(MEMBER_TOTAL, NLAT, LON)
```

```python
import functools
import math

import jax
import jax.numpy as jnp
from jax import lax
from jax.experimental import pallas as pl
from jax.experimental.pallas import tpu as pltpu
from jax.sharding import PartitionSpec as P

STEPS = 4
NS_ITERS = 4
REGION_VALUES = 256
TILE = 8

step_size = 0.05
coupling = 0.4

MESH = pl.DeviceIdType.MESH
bf16 = jnp.bfloat16
f32 = jnp.float32


def split(x):
    hi = x.astype(bf16)
    lo = (x - hi.astype(f32)).astype(bf16)
    return hi, lo


def dot(a, b):
    return lax.dot_general(a, b, (((1,), (0,)), ((), ())), preferred_element_type=f32)


def wide_lhs(x):
    return jnp.concatenate(split(x), axis=1)


def small_rhs(x):
    both = jnp.concatenate(split(x), axis=1)
    return jnp.concatenate([both, both], axis=0)


def small_dot(lhs_parts, rhs):
    size = rhs.shape[0]
    lhs = jnp.concatenate([wide_lhs(part) for part in lhs_parts], axis=0)
    both = dot(lhs, small_rhs(rhs))
    total = both[:, :size] + both[:, size:]
    return [total[size * k : size * (k + 1)] for k in range(len(lhs_parts))]


def kernel(
    n_mem,
    n_strip,
    members,
    count_ref,
    x_ref,
    index_ref,
    value_ref,
    prec_ref,
    out_ref,
    halo,
    fc,
    rbuf,
    ana,
    bt_ref,
    e_ref,
    hsend,
    hrecv,
    asend,
    arecv,
    bsend,
    brecv,
):
    rows, padded_members, lon = x_ref.shape
    groups, obs = index_ref.shape
    chunks = asend.shape[0]
    per_chunk = members // chunks
    total = members * n_mem
    me = lax.axis_index("mem")
    strip = lax.axis_index("strip")
    has_low = strip > 0
    has_high = strip < n_strip - 1

    def place(owner, i):
        flat = (owner * groups + i) * REGION_VALUES
        return flat // lon, pl.multiple_of(flat % lon, REGION_VALUES)

    barrier = pltpu.get_barrier_semaphore()
    for d in range(1, n_mem):
        pl.semaphore_signal(
            barrier, inc=1, device_id=(lax.rem(me + d, n_mem), strip), device_id_type=MESH
        )

    @pl.when(has_low)
    def _():
        pl.semaphore_signal(barrier, inc=1, device_id=(me, strip - 1), device_id_type=MESH)

    @pl.when(has_high)
    def _():
        pl.semaphore_signal(barrier, inc=1, device_id=(me, strip + 1), device_id_type=MESH)

    pl.semaphore_wait(
        barrier, n_mem - 1 + jnp.where(has_low, 1, 0) + jnp.where(has_high, 1, 0)
    )

    def halo_copy(side):
        return pltpu.make_async_remote_copy(
            src_ref=x_ref.at[pl.ds(rows - STEPS if side == 0 else 0, STEPS)],
            dst_ref=halo.at[side],
            send_sem=hsend.at[side],
            recv_sem=hrecv.at[side],
            device_id=(me, strip + 1 if side == 0 else strip - 1),
            device_id_type=MESH,
        )

    sends = (has_high, has_low)
    receives = (has_low, has_high)
    for side in range(2):

        @pl.when(sends[side])
        def _(side=side):
            halo_copy(side).start()

        @pl.when(jnp.logical_not(receives[side]))
        def _(side=side):
            halo[side] = jnp.zeros(halo.shape[1:], f32)

    for side in range(2):

        @pl.when(receives[side])
        def _(side=side):
            halo_copy(side).wait_recv()

    low_in = jnp.where(has_low, 1.0, 0.0).astype(f32)
    high_in = jnp.where(has_high, 1.0, 0.0).astype(f32)

    def stacked(r, at):
        if r < STEPS:
            return halo[0, r, at, :]
        if r < STEPS + rows:
            return x_ref[r - STEPS, at, :]
        return halo[1, r - STEPS - rows, at, :]

    def march(tile):
        at = pl.ds(pl.multiple_of(tile * TILE, TILE), TILE)
        force_at = pl.ds(members, TILE)
        state = [stacked(r, at) for r in range(rows + 2 * STEPS)]
        first = 0
        for _ in range(STEPS):
            following = []
            for k in range(1, len(state) - 1):
                r = first + k
                u = state[k]
                advection = (pltpu.roll(u, lon - 1, 1) - pltpu.roll(u, 2, 1)) * pltpu.roll(u, 1, 1)
                new = (
                    (1.0 - step_size - 2.0 * coupling) * u
                    + step_size * (advection + stacked(r, force_at))
                    + coupling * (state[k - 1] + state[k + 1])
                )
                if r < STEPS:
                    new = new * low_in
                elif r >= STEPS + rows:
                    new = new * high_in
                following.append(new)
            state = following
            first += 1
        for r in range(rows):
            fc[r, at, :] = state[r]

    def out_copy(c, d, i):
        peer = lax.rem(me + d, n_mem)
        row, col = place(peer, i)
        at = pl.ds(c * per_chunk, per_chunk)
        return pltpu.make_async_remote_copy(
            src_ref=fc.at[row, at, pl.ds(col, REGION_VALUES)],
            dst_ref=rbuf.at[i, pl.ds(me * members + c * per_chunk, per_chunk), :],
            send_sem=asend.at[c, d - 1, i],
            recv_sem=arecv.at[c, d - 1, i],
            device_id=(peer, strip),
            device_id_type=MESH,
        )

    tiles = per_chunk // TILE
    for c in range(chunks):

        def body(t, carry, c=c):
            march(c * tiles + t)
            return carry

        lax.fori_loop(0, tiles, body, 0)
        for i in range(groups):
            for d in range(1, n_mem):
                out_copy(c, d, i).start()

    own = pl.ds(pl.multiple_of(me * members, TILE), members)
    for i in range(groups):
        row, col = place(me, i)
        rbuf[i, own, :] = fc[row, :, pl.ds(col, REGION_VALUES)]

    eye = (
        lax.broadcasted_iota(jnp.int32, (obs, obs), 0)
        == lax.broadcasted_iota(jnp.int32, (obs, obs), 1)
    ).astype(f32)
    spread_dof = float(total - 1)

    def prepare(i):
        for c in range(chunks):
            for d in range(1, n_mem):
                out_copy(c, d, i).wait_recv()
        values = rbuf[i]
        mean = jnp.sum(values, axis=0, keepdims=True) * (1.0 / total)
        spread = values - mean
        rbuf[i] = spread
        s_hi, s_lo = split(spread)
        onehot = (
            lax.broadcasted_iota(jnp.int32, (REGION_VALUES, obs), 0) == index_ref[i : i + 1, :]
        ).astype(f32).astype(bf16)
        both = dot(jnp.concatenate([s_hi, s_lo], axis=0), onehot)
        obs_spread = both[:total] + both[total:]
        m_hi = mean.astype(bf16)
        rest = mean - m_hi.astype(f32)
        m_mid = rest.astype(bf16)
        m_lo = (rest - m_mid.astype(f32)).astype(bf16)
        mean_rows = [jnp.broadcast_to(p, (16, REGION_VALUES)) for p in (m_hi, m_mid, m_lo)]
        picked = dot(jnp.concatenate(mean_rows, axis=0), onehot)
        obs_mean = picked[0:1] + picked[16:17] + picked[32:33]
        slots = lax.broadcasted_iota(jnp.int32, (1, obs), 1)
        weight = jnp.where(slots < count_ref[i], prec_ref[i : i + 1, :], 0.0)
        root = jnp.sqrt(weight)
        u_row = root * (value_ref[i : i + 1, :] - obs_mean)
        u_col = jnp.sum(eye * u_row, axis=1, keepdims=True)
        bt = obs_spread * root
        b = bt.T
        bt_wide = wide_lhs(bt)
        bt_ref[i] = bt_wide
        b_hi, b_lo = split(b)
        b_tall = jnp.concatenate([b_hi, b_lo], axis=0)
        k4 = dot(b_tall, bt_wide)
        gram = (k4[:obs, :obs] + k4[obs:, obs:]) + (k4[:obs, obs:] + k4[obs:, :obs])
        e2 = dot(b_tall, s_hi)
        e_ref[i] = e2[:obs] + e2[obs:] + dot(b_hi, s_lo)
        return mean, gram, u_col

    prepared = [prepare(i) for i in range(groups)]

    def invert(gram):
        squares = jnp.sum(jnp.sum(gram * gram, axis=0, keepdims=True), axis=1, keepdims=True)
        scale = spread_dof + jnp.sqrt(squares)
        inv = 1.0 / scale
        a0 = spread_dof * inv
        left = a0 * eye + inv * gram
        right = 1.5 * eye - 0.5 * left
        r0 = 1.5 - 0.5 * a0
        l0 = a0 * r0
        rq = None
        rq_scalar = -0.5 * inv
        (left,) = small_dot([left], right)
        for it in range(1, NS_ITERS):
            if rq is None:
                (product,) = small_dot([right], left)
                lq = inv * right + (a0 * rq_scalar) * eye
                pq = rq_scalar * left + r0 * lq
            else:
                product, rq_left = small_dot([right, rq], left)
                lq = inv * right + a0 * rq
                pq = rq_left + r0 * lq
            corr = 1.5 * eye - 0.5 * product
            cq = -0.5 * pq
            c0 = 1.5 - 0.5 * r0 * l0
            last = it == NS_ITERS - 1
            if rq is None:
                rq = rq_scalar * corr + r0 * cq
                left, right = small_dot([left, right], corr)
            elif last:
                right, moved = small_dot([right, rq], corr)
                rq = moved + r0 * cq
            else:
                left, right, moved = small_dot([left, right, rq], corr)
                rq = moved + r0 * cq
            r0, l0 = r0 * c0, l0 * c0
        return scale, right, r0, rq

    inverted = [invert(gram) for _, gram, _ in prepared]

    def back_copy(d, i):
        peer = lax.rem(me + d, n_mem)
        row, col = place(me, i)
        return pltpu.make_async_remote_copy(
            src_ref=ana.at[i, pl.ds(pl.multiple_of(peer * members, TILE), members), :],
            dst_ref=out_ref.at[row, :, pl.ds(col, REGION_VALUES)],
            send_sem=bsend.at[d - 1, i],
            recv_sem=brecv.at[d - 1, i],
            device_id=(peer, strip),
            device_id_type=MESH,
        )

    for i in range(groups):
        mean, _, u_col = prepared[i]
        scale, right, r0, rq = inverted[i]
        amp = math.sqrt(spread_dof) / jnp.sqrt(scale)
        e = e_ref[i]
        e_hi, e_lo = split(e)
        rq_wide = wide_lhs(amp * rq)
        z = dot(rq_wide, jnp.concatenate([e_hi, e_hi], axis=0)) + dot(
            rq_wide, jnp.concatenate([e_lo, e_lo], axis=0)
        )
        w1 = jnp.sum(u_col * right, axis=0, keepdims=True)
        w2 = jnp.sum(right * w1, axis=1, keepdims=True) / scale
        shift = mean + jnp.sum(w2 * e, axis=0, keepdims=True)
        z_hi, z_lo = split(z)
        bt_wide = bt_ref[i]
        moved = dot(bt_wide, jnp.concatenate([z_hi, z_hi], axis=0)) + dot(
            bt_wide, jnp.concatenate([z_lo, z_lo], axis=0)
        )
        ana[i] = moved + (amp * r0) * rbuf[i] + shift
        for d in range(1, n_mem):
            back_copy(d, i).start()
        row, col = place(me, i)
        out_ref[row, :, pl.ds(col, REGION_VALUES)] = ana[i, own, :]

    for side in range(2):

        @pl.when(sends[side])
        def _(side=side):
            halo_copy(side).wait_send()

    for c in range(chunks):
        for i in range(groups):
            for d in range(1, n_mem):
                out_copy(c, d, i).wait_send()
    for i in range(groups):
        for d in range(1, n_mem):
            back_copy(d, i).wait()


def local(n_mem, n_strip, ensemble, forcing, obs_index, obs_count, obs_value, obs_precision):
    members, rows, lon = ensemble.shape
    groups, obs = obs_index.shape
    total = members * n_mem
    chunks = max(1, members // (2 * TILE))
    x = jnp.concatenate(
        [
            jnp.transpose(ensemble, (1, 0, 2)),
            jnp.broadcast_to(forcing[:, None, :], (rows, TILE, lon)),
        ],
        axis=1,
    )
    vmem = pl.BlockSpec(memory_space=pltpu.VMEM)
    dma = pltpu.SemaphoreType.DMA
    out = pl.pallas_call(
        functools.partial(kernel, n_mem, n_strip, members),
        out_shape=jax.ShapeDtypeStruct((rows, members, lon), f32),
        in_specs=[pl.BlockSpec(memory_space=pltpu.SMEM)] + [vmem] * 4,
        out_specs=vmem,
        scratch_shapes=[
            pltpu.VMEM((2, STEPS, members + TILE, lon), f32),
            pltpu.VMEM((rows, members, lon), f32),
            pltpu.VMEM((groups, total, REGION_VALUES), f32),
            pltpu.VMEM((groups, total, REGION_VALUES), f32),
            pltpu.VMEM((groups, total, 2 * obs), bf16),
            pltpu.VMEM((groups, obs, REGION_VALUES), f32),
            dma((2,)),
            dma((2,)),
            dma((chunks, n_mem - 1, groups)),
            dma((chunks, n_mem - 1, groups)),
            dma((n_mem - 1, groups)),
            dma((n_mem - 1, groups)),
        ],
        compiler_params=pltpu.CompilerParams(
            collective_id=0, has_side_effects=True, vmem_limit_bytes=48 * 1024 * 1024
        ),
    )(obs_count, x, obs_index, obs_value, obs_precision)
    return jnp.transpose(out, (1, 0, 2))


def solution(mesh):
    placed = (
        P("mem", "strip", None),
        P("strip", None),
        P(("strip", "mem"), None),
        P(("strip", "mem")),
        P(("strip", "mem"), None),
        P(("strip", "mem"), None),
    )
    return jax.shard_map(
        functools.partial(local, mesh.shape["mem"], mesh.shape["strip"]),
        mesh=mesh,
        in_specs=placed,
        out_specs=P("mem", "strip", None),
        check_vma=False,
    )
```

```python
import functools
import math

import jax
import jax.numpy as jnp
from jax import lax
from jax.experimental import pallas as pl
from jax.experimental.pallas import tpu as pltpu
from jax.sharding import PartitionSpec as P

STEPS = 4
NS_ITERS = 4
REGION_VALUES = 256
TILE = 8
LANES = 128

step_size = 0.05
coupling = 0.4

MESH = pl.DeviceIdType.MESH
bf16 = jnp.bfloat16
f32 = jnp.float32


def split(x):
    hi = x.astype(bf16)
    lo = (x - hi.astype(f32)).astype(bf16)
    return hi, lo


def dot(a, b):
    return lax.dot_general(a, b, (((1,), (0,)), ((), ())), preferred_element_type=f32)


def wide_lhs(x):
    return jnp.concatenate(split(x), axis=1)


def small_rhs(x):
    both = jnp.concatenate(split(x), axis=1)
    return jnp.concatenate([both, both], axis=0)


def small_dot(lhs_parts, rhs):
    size = rhs.shape[0]
    lhs = jnp.concatenate([wide_lhs(part) for part in lhs_parts], axis=0)
    both = dot(lhs, small_rhs(rhs))
    total = both[:, :size] + both[:, size:]
    return [total[size * k : size * (k + 1)] for k in range(len(lhs_parts))]


def kernel(
    n_mem,
    n_strip,
    members,
    ens_hbm,
    forcing_hbm,
    index_hbm,
    count_hbm,
    value_hbm,
    prec_hbm,
    out_ref,
    count_ref,
    index_ref,
    value_ref,
    prec_ref,
    x_ref,
    halo,
    forcing_ref,
    pushed,
    fc,
    rbuf,
    ana,
    bt_ref,
    e_ref,
    hsend,
    hrecv,
    asend,
    arecv,
    bsend,
    brecv,
    fsend,
    frecv,
    lsem,
):
    lanes, _, rows, _ = x_ref.shape
    lon = lanes * LANES
    groups, obs = index_ref.shape
    chunks = asend.shape[0]
    per_chunk = members // chunks
    total = members * n_mem
    me = lax.axis_index("mem")
    strip = lax.axis_index("strip")
    has_low = strip > 0
    has_high = strip < n_strip - 1

    def place(owner, i):
        flat = (owner * groups + i) * REGION_VALUES
        return flat // lon, pl.multiple_of(flat % lon, REGION_VALUES)

    moves = [(ens_hbm.at[:, :, pl.ds(h * LANES, LANES)], x_ref.at[h]) for h in range(lanes)]
    moves += [
        (forcing_hbm, forcing_ref.at[1]),
        (index_hbm, index_ref),
        (value_hbm, value_ref),
        (prec_hbm, prec_ref),
        (count_hbm, count_ref),
    ]
    loads = [pltpu.make_async_copy(*move, lsem.at[k]) for k, move in enumerate(moves)]
    for load in loads:
        load.start()

    barrier = pltpu.get_barrier_semaphore()
    for d in range(1, n_mem):
        pl.semaphore_signal(
            barrier, inc=1, device_id=(lax.rem(me + d, n_mem), strip), device_id_type=MESH
        )

    @pl.when(has_low)
    def _():
        pl.semaphore_signal(barrier, inc=1, device_id=(me, strip - 1), device_id_type=MESH)

    @pl.when(has_high)
    def _():
        pl.semaphore_signal(barrier, inc=1, device_id=(me, strip + 1), device_id_type=MESH)

    pl.semaphore_wait(
        barrier, n_mem - 1 + jnp.where(has_low, 1, 0) + jnp.where(has_high, 1, 0)
    )

    def halo_side(side):
        at = pl.ds(rows - STEPS if side == 0 else 0, STEPS)
        return at, (me, strip + 1 if side == 0 else strip - 1)

    def halo_copies(side, c):
        at, target = halo_side(side)
        part = pl.ds(c * per_chunk, per_chunk)
        return [
            pltpu.make_async_remote_copy(
                src_ref=ens_hbm.at[part, at, pl.ds(h * LANES, LANES)],
                dst_ref=halo.at[h, part, at, :],
                send_sem=hsend.at[side, c, h],
                recv_sem=hrecv.at[side, c, h],
                device_id=target,
                device_id_type=MESH,
            )
            for h in range(lanes)
        ]

    def forcing_copy(side):
        return pltpu.make_async_remote_copy(
            src_ref=forcing_hbm,
            dst_ref=forcing_ref.at[2 * side],
            send_sem=fsend.at[side],
            recv_sem=frecv.at[side],
            device_id=halo_side(side)[1],
            device_id_type=MESH,
        )

    def all_halo_copies(side):
        parts = [copy for c in range(chunks) for copy in halo_copies(side, c)]
        return [forcing_copy(side)] + parts

    sends = (has_high, has_low)
    receives = (has_low, has_high)
    for side in range(2):

        @pl.when(sends[side])
        def _(side=side):
            for copy in all_halo_copies(side):
                copy.start()

        @pl.when(jnp.logical_not(receives[side]))
        def _(side=side):
            at, _ = halo_side(side)
            halo[:, :, at, :] = jnp.zeros((lanes, members, STEPS, LANES), f32)
            forcing_ref[2 * side] = jnp.zeros((rows, lon), f32)

    for load in loads:
        load.wait()
    for side in range(2):

        @pl.when(receives[side])
        def _(side=side):
            forcing_copy(side).wait_recv()

    low_in = jnp.where(has_low, 1.0, 0.0).astype(f32)
    high_in = jnp.where(has_high, 1.0, 0.0).astype(f32)

    x_flat = x_ref.reshape(lanes * members * rows, LANES)
    halo_flat = halo.reshape(lanes * members * rows, LANES)
    for r in range(1, rows + 2 * STEPS - 1):
        side, row = divmod(r - STEPS + rows, rows)
        pushed[r] = jnp.broadcast_to(step_size * forcing_ref[side, row : row + 1, :], (TILE, lon))

    def march(tile):
        at = pl.ds(pl.multiple_of(tile * TILE, TILE), TILE)

        def row_of(r):
            side, row = divmod(r - STEPS + rows, rows)
            source = x_flat if side == 1 else halo_flat
            starts = [(h * members + tile * TILE) * rows + row for h in range(lanes)]
            return jnp.concatenate(
                [source[pl.ds(start, TILE, stride=rows), :] for start in starts], axis=1
            )

        state = [row_of(r) for r in range(rows + 2 * STEPS)]
        first = 0
        for _ in range(STEPS):
            following = []
            for k in range(1, len(state) - 1):
                r = first + k
                u = state[k]
                advection = (pltpu.roll(u, lon - 1, 1) - pltpu.roll(u, 2, 1)) * pltpu.roll(u, 1, 1)
                new = (
                    (1.0 - step_size - 2.0 * coupling) * u
                    + (step_size * advection + pushed[r])
                    + coupling * (state[k - 1] + state[k + 1])
                )
                if r < STEPS:
                    new = new * low_in
                elif r >= STEPS + rows:
                    new = new * high_in
                following.append(new)
            state = following
            first += 1
        for r in range(rows):
            fc[r, at, :] = state[r]

    def out_copy(c, d, i):
        peer = lax.rem(me + d, n_mem)
        row, col = place(peer, i)
        at = pl.ds(c * per_chunk, per_chunk)
        return pltpu.make_async_remote_copy(
            src_ref=fc.at[row, at, pl.ds(col, REGION_VALUES)],
            dst_ref=rbuf.at[i, pl.ds(me * members + c * per_chunk, per_chunk), :],
            send_sem=asend.at[c, d - 1, i],
            recv_sem=arecv.at[c, d - 1, i],
            device_id=(peer, strip),
            device_id_type=MESH,
        )

    tiles = per_chunk // TILE
    for c in range(chunks):
        for side in range(2):

            @pl.when(receives[side])
            def _(side=side, c=c):
                for copy in halo_copies(side, c):
                    copy.wait_recv()

        def body(t, carry, c=c):
            march(c * tiles + t)
            return carry

        lax.fori_loop(0, tiles, body, 0)
        for d in range(1, n_mem):
            out_copy(c, d, 0).start()
    for i in range(1, groups):
        for c in range(chunks):
            for d in range(1, n_mem):
                out_copy(c, d, i).start()

    own = pl.ds(pl.multiple_of(me * members, TILE), members)
    for i in range(groups):
        row, col = place(me, i)
        rbuf[i, own, :] = fc[row, :, pl.ds(col, REGION_VALUES)]

    eye = (
        lax.broadcasted_iota(jnp.int32, (obs, obs), 0)
        == lax.broadcasted_iota(jnp.int32, (obs, obs), 1)
    ).astype(f32)
    spread_dof = float(total - 1)

    def prepare(i):
        for c in range(chunks):
            for d in range(1, n_mem):
                out_copy(c, d, i).wait_recv()
        values = rbuf[i]
        mean = jnp.sum(values, axis=0, keepdims=True) * (1.0 / total)
        spread = values - mean
        rbuf[i] = spread
        s_hi, s_lo = split(spread)
        onehot = (
            lax.broadcasted_iota(jnp.int32, (REGION_VALUES, obs), 0) == index_ref[i : i + 1, :]
        ).astype(f32).astype(bf16)
        both = dot(jnp.concatenate([s_hi, s_lo], axis=0), onehot)
        obs_spread = both[:total] + both[total:]
        m_hi = mean.astype(bf16)
        rest = mean - m_hi.astype(f32)
        m_mid = rest.astype(bf16)
        m_lo = (rest - m_mid.astype(f32)).astype(bf16)
        mean_rows = [jnp.broadcast_to(p, (16, REGION_VALUES)) for p in (m_hi, m_mid, m_lo)]
        picked = dot(jnp.concatenate(mean_rows, axis=0), onehot)
        obs_mean = picked[0:1] + picked[16:17] + picked[32:33]
        slots = lax.broadcasted_iota(jnp.int32, (1, obs), 1)
        weight = jnp.where(slots < count_ref[0:1, i : i + 1], prec_ref[i : i + 1, :], 0.0)
        root = jnp.sqrt(weight)
        u_row = root * (value_ref[i : i + 1, :] - obs_mean)
        u_col = jnp.sum(eye * u_row, axis=1, keepdims=True)
        bt = obs_spread * root
        b = bt.T
        bt_wide = wide_lhs(bt)
        bt_ref[i] = bt_wide
        b_hi, b_lo = split(b)
        b_tall = jnp.concatenate([b_hi, b_lo], axis=0)
        k4 = dot(b_tall, bt_wide)
        gram = (k4[:obs, :obs] + k4[obs:, obs:]) + (k4[:obs, obs:] + k4[obs:, :obs])
        e2 = dot(b_tall, s_hi)
        e_ref[i] = e2[:obs] + e2[obs:] + dot(b_hi, s_lo)
        return mean, gram, u_col


    def invert(gram):
        squares = jnp.sum(jnp.sum(gram * gram, axis=0, keepdims=True), axis=1, keepdims=True)
        scale = spread_dof + jnp.sqrt(squares)
        inv = 1.0 / scale
        a0 = spread_dof * inv
        left = a0 * eye + inv * gram
        right = 1.5 * eye - 0.5 * left
        r0 = 1.5 - 0.5 * a0
        l0 = a0 * r0
        rq = None
        rq_scalar = -0.5 * inv
        (left,) = small_dot([left], right)
        for it in range(1, NS_ITERS):
            if rq is None:
                (product,) = small_dot([right], left)
                lq = inv * right + (a0 * rq_scalar) * eye
                pq = rq_scalar * left + r0 * lq
            else:
                product, rq_left = small_dot([right, rq], left)
                lq = inv * right + a0 * rq
                pq = rq_left + r0 * lq
            corr = 1.5 * eye - 0.5 * product
            cq = -0.5 * pq
            c0 = 1.5 - 0.5 * r0 * l0
            last = it == NS_ITERS - 1
            if rq is None:
                rq = rq_scalar * corr + r0 * cq
                left, right = small_dot([left, right], corr)
            elif last:
                right, moved = small_dot([right, rq], corr)
                rq = moved + r0 * cq
            else:
                left, right, moved = small_dot([left, right, rq], corr)
                rq = moved + r0 * cq
            r0, l0 = r0 * c0, l0 * c0
        return scale, right, r0, rq


    def back_copy(d, i):
        peer = lax.rem(me + d, n_mem)
        row, col = place(me, i)
        return pltpu.make_async_remote_copy(
            src_ref=ana.at[i, pl.ds(pl.multiple_of(peer * members, TILE), members), :],
            dst_ref=out_ref.at[row, :, pl.ds(col, REGION_VALUES)],
            send_sem=bsend.at[d - 1, i],
            recv_sem=brecv.at[d - 1, i],
            device_id=(peer, strip),
            device_id_type=MESH,
        )

    for i in range(groups):
        mean, gram, u_col = prepare(i)
        scale, right, r0, rq = invert(gram)
        amp = math.sqrt(spread_dof) / jnp.sqrt(scale)
        e = e_ref[i]
        e_hi, e_lo = split(e)
        rq_wide = wide_lhs(amp * rq)
        z = dot(rq_wide, jnp.concatenate([e_hi, e_hi], axis=0)) + dot(
            rq_wide, jnp.concatenate([e_lo, e_lo], axis=0)
        )
        w1 = jnp.sum(u_col * right, axis=0, keepdims=True)
        w2 = jnp.sum(right * w1, axis=1, keepdims=True) / scale
        shift = mean + jnp.sum(w2 * e, axis=0, keepdims=True)
        z_hi, z_lo = split(z)
        bt_wide = bt_ref[i]
        moved = dot(bt_wide, jnp.concatenate([z_hi, z_hi], axis=0)) + dot(
            bt_wide, jnp.concatenate([z_lo, z_lo], axis=0)
        )
        ana[i] = moved + (amp * r0) * rbuf[i] + shift
        for d in range(1, n_mem):
            back_copy(d, i).start()
        row, col = place(me, i)
        out_ref[row, :, pl.ds(col, REGION_VALUES)] = ana[i, own, :]

    for side in range(2):

        @pl.when(sends[side])
        def _(side=side):
            for copy in all_halo_copies(side):
                copy.wait_send()

    for c in range(chunks):
        for i in range(groups):
            for d in range(1, n_mem):
                out_copy(c, d, i).wait_send()
    for i in range(groups):
        for d in range(1, n_mem):
            back_copy(d, i).wait()


def local(n_mem, n_strip, ensemble, forcing, obs_index, obs_count, obs_value, obs_precision):
    members, rows, lon = ensemble.shape
    groups, obs = obs_index.shape
    total = members * n_mem
    lanes = lon // LANES
    chunks = max(1, members // (2 * TILE))
    vmem = pl.BlockSpec(memory_space=pltpu.VMEM)
    dma = pltpu.SemaphoreType.DMA
    out = pl.pallas_call(
        functools.partial(kernel, n_mem, n_strip, members),
        out_shape=jax.ShapeDtypeStruct((rows, members, lon), f32),
        in_specs=[pl.BlockSpec(memory_space=pl.ANY)] * 6,
        out_specs=vmem,
        scratch_shapes=[
            pltpu.VMEM((1, groups), jnp.int32),
            pltpu.VMEM((groups, obs), jnp.int32),
            pltpu.VMEM((groups, obs), f32),
            pltpu.VMEM((groups, obs), f32),
            pltpu.VMEM((lanes, members, rows, LANES), f32),
            pltpu.VMEM((lanes, members, rows, LANES), f32),
            pltpu.VMEM((3, rows, lon), f32),
            pltpu.VMEM((rows + 2 * STEPS, TILE, lon), f32),
            pltpu.VMEM((rows, members, lon), f32),
            pltpu.VMEM((groups, total, REGION_VALUES), f32),
            pltpu.VMEM((groups, total, REGION_VALUES), f32),
            pltpu.VMEM((groups, total, 2 * obs), bf16),
            pltpu.VMEM((groups, obs, REGION_VALUES), f32),
            dma((2, chunks, lanes)),
            dma((2, chunks, lanes)),
            dma((chunks, n_mem - 1, groups)),
            dma((chunks, n_mem - 1, groups)),
            dma((n_mem - 1, groups)),
            dma((n_mem - 1, groups)),
            dma((2,)),
            dma((2,)),
            dma((lanes + 5,)),
        ],
        compiler_params=pltpu.CompilerParams(
            collective_id=0, has_side_effects=True, vmem_limit_bytes=67043328
        ),
    )(ensemble, forcing, obs_index, obs_count[None], obs_value, obs_precision)
    return jnp.transpose(out, (1, 0, 2))


def solution(mesh):
    placed = (
        P("mem", "strip", None),
        P("strip", None),
        P(("strip", "mem"), None),
        P(("strip", "mem")),
        P(("strip", "mem"), None),
        P(("strip", "mem"), None),
    )
    return jax.shard_map(
        functools.partial(local, mesh.shape["mem"], mesh.shape["strip"]),
        mesh=mesh,
        in_specs=placed,
        out_specs=P("mem", "strip", None),
        check_vma=False,
    )
```

```python
import functools
import math

import jax
import jax.numpy as jnp
from jax import lax
from jax.experimental import pallas as pl
from jax.experimental.pallas import tpu as pltpu
from jax.sharding import PartitionSpec as P

STEPS = 4
NS_ITERS = 4
REGION_VALUES = 256
TILE = 8
LANES = 128

step_size = 0.05
coupling = 0.4

MESH = pl.DeviceIdType.MESH
bf16 = jnp.bfloat16
f32 = jnp.float32


def split(x):
    hi = x.astype(bf16)
    lo = (x - hi.astype(f32)).astype(bf16)
    return hi, lo


def dot(a, b):
    return lax.dot_general(a, b, (((1,), (0,)), ((), ())), preferred_element_type=f32)


def wide_lhs(x):
    return jnp.concatenate(split(x), axis=1)


def small_rhs(x):
    both = jnp.concatenate(split(x), axis=1)
    return jnp.concatenate([both, both], axis=0)


def small_dot(lhs_parts, rhs):
    size = rhs.shape[0]
    lhs = jnp.concatenate([wide_lhs(part) for part in lhs_parts], axis=0)
    both = dot(lhs, small_rhs(rhs))
    total = both[:, :size] + both[:, size:]
    return [total[size * k : size * (k + 1)] for k in range(len(lhs_parts))]


def kernel(
    n_mem,
    n_strip,
    members,
    ens_hbm,
    forcing_hbm,
    index_hbm,
    count_hbm,
    value_hbm,
    prec_hbm,
    out_ref,
    count_ref,
    index_ref,
    value_ref,
    prec_ref,
    x_ref,
    halo,
    forcing_ref,
    pushed,
    mid,
    fc,
    rbuf,
    ana,
    bt_ref,
    e_ref,
    hsend,
    hrecv,
    asend,
    arecv,
    bsend,
    brecv,
    fsend,
    frecv,
    lsem,
):
    lanes, _, rows, _ = x_ref.shape
    lon = lanes * LANES
    groups, obs = index_ref.shape
    chunks = asend.shape[0]
    per_chunk = members // chunks
    total = members * n_mem
    me = lax.axis_index("mem")
    strip = lax.axis_index("strip")
    has_low = strip > 0
    has_high = strip < n_strip - 1

    def place(owner, i):
        flat = (owner * groups + i) * REGION_VALUES
        return flat // lon, pl.multiple_of(flat % lon, REGION_VALUES)

    moves = [(ens_hbm.at[:, :, pl.ds(h * LANES, LANES)], x_ref.at[h]) for h in range(lanes)]
    moves += [
        (forcing_hbm, forcing_ref.at[1]),
        (index_hbm, index_ref),
        (value_hbm, value_ref),
        (prec_hbm, prec_ref),
        (count_hbm, count_ref),
    ]
    loads = [pltpu.make_async_copy(*move, lsem.at[k]) for k, move in enumerate(moves)]
    for load in loads:
        load.start()

    barrier = pltpu.get_barrier_semaphore()
    for d in range(1, n_mem):
        pl.semaphore_signal(
            barrier, inc=1, device_id=(lax.rem(me + d, n_mem), strip), device_id_type=MESH
        )

    @pl.when(has_low)
    def _():
        pl.semaphore_signal(barrier, inc=1, device_id=(me, strip - 1), device_id_type=MESH)

    @pl.when(has_high)
    def _():
        pl.semaphore_signal(barrier, inc=1, device_id=(me, strip + 1), device_id_type=MESH)

    pl.semaphore_wait(
        barrier, n_mem - 1 + jnp.where(has_low, 1, 0) + jnp.where(has_high, 1, 0)
    )

    def halo_side(side):
        at = pl.ds(rows - STEPS if side == 0 else 0, STEPS)
        return at, (me, strip + 1 if side == 0 else strip - 1)

    def halo_copies(side, c):
        at, target = halo_side(side)
        part = pl.ds(c * per_chunk, per_chunk)
        return [
            pltpu.make_async_remote_copy(
                src_ref=ens_hbm.at[part, at, pl.ds(h * LANES, LANES)],
                dst_ref=halo.at[h, part, at, :],
                send_sem=hsend.at[side, c, h],
                recv_sem=hrecv.at[side, c, h],
                device_id=target,
                device_id_type=MESH,
            )
            for h in range(lanes)
        ]

    def forcing_copy(side):
        return pltpu.make_async_remote_copy(
            src_ref=forcing_hbm,
            dst_ref=forcing_ref.at[2 * side],
            send_sem=fsend.at[side],
            recv_sem=frecv.at[side],
            device_id=halo_side(side)[1],
            device_id_type=MESH,
        )

    def all_halo_copies(side):
        parts = [copy for c in range(chunks) for copy in halo_copies(side, c)]
        return [forcing_copy(side)] + parts

    sends = (has_high, has_low)
    receives = (has_low, has_high)
    for side in range(2):

        @pl.when(sends[side])
        def _(side=side):
            for copy in all_halo_copies(side):
                copy.start()

        @pl.when(jnp.logical_not(receives[side]))
        def _(side=side):
            at, _ = halo_side(side)
            halo[:, :, at, :] = jnp.zeros((lanes, members, STEPS, LANES), f32)
            forcing_ref[2 * side] = jnp.zeros((rows, lon), f32)

    for load in loads:
        load.wait()
    low_in = jnp.where(has_low, 1.0, 0.0).astype(f32)
    high_in = jnp.where(has_high, 1.0, 0.0).astype(f32)

    x_flat = x_ref.reshape(lanes * members * rows, LANES)
    halo_flat = halo.reshape(lanes * members * rows, LANES)
    def push(ext_rows):
        for r in ext_rows:
            side, row = divmod(r - STEPS + rows, rows)
            pushed[r] = jnp.broadcast_to(
                step_size * forcing_ref[side, row : row + 1, :], (TILE, lon)
            )

    def inner(step, row):
        return 0 < step < STEPS and step <= row < rows - step

    def kept(step, row):
        return inner(step, row) and not inner(step + 1, row - 1) or (
            inner(step, row) and not (inner(step + 1, row) and inner(step + 1, row + 1))
        )

    slots = [(s, r) for s in range(1, STEPS) for r in range(rows) if kept(s, r)]

    def advance(above, u, below, row):
        advection = (pltpu.roll(u, lon - 1, 1) - pltpu.roll(u, 2, 1)) * pltpu.roll(u, 1, 1)
        new = (
            (1.0 - step_size - 2.0 * coupling) * u
            + (step_size * advection + pushed[row + STEPS])
            + coupling * (above + below)
        )
        if row < 0:
            new = new * low_in
        elif row >= rows:
            new = new * high_in
        return new

    def row_of(tile, row):
        side, row = divmod(row + rows, rows)
        source = x_flat if side == 1 else halo_flat
        starts = [(h * members + tile * TILE) * rows + row for h in range(lanes)]
        return jnp.concatenate(
            [source[pl.ds(start, TILE, stride=rows), :] for start in starts], axis=1
        )

    def tile_at(tile):
        return pl.ds(pl.multiple_of(tile * TILE, TILE), TILE)

    def march_inner(tile):
        current = {r: row_of(tile, r) for r in range(rows)}
        for step in range(1, STEPS):
            current = {
                r: advance(current[r - 1], current[r], current[r + 1], r)
                for r in range(rows)
                if inner(step, r)
            }
            for r in current:
                if (step, r) in slots:
                    mid[slots.index((step, r)), tile_at(tile), :] = current[r]

    def march_outer(tile):
        current = {}

        def value(step, r):
            if r not in current:
                if step == 0:
                    current[r] = row_of(tile, r)
                else:
                    current[r] = mid[slots.index((step, r)), tile_at(tile), :]
            return current[r]

        for step in range(1, STEPS + 1):
            reach = STEPS - step
            current = {
                r: advance(*(value(step - 1, r + k) for k in (-1, 0, 1)), r)
                for r in range(-reach, rows + reach)
                if not inner(step, r)
            }
        for r in range(rows):
            fc[r, tile_at(tile), :] = current[r]

    def out_copy(c, d, i):
        peer = lax.rem(me + d, n_mem)
        row, col = place(peer, i)
        at = pl.ds(c * per_chunk, per_chunk)
        return pltpu.make_async_remote_copy(
            src_ref=fc.at[row, at, pl.ds(col, REGION_VALUES)],
            dst_ref=rbuf.at[i, pl.ds(me * members + c * per_chunk, per_chunk), :],
            send_sem=asend.at[c, d - 1, i],
            recv_sem=arecv.at[c, d - 1, i],
            device_id=(peer, strip),
            device_id_type=MESH,
        )

    push(range(STEPS, STEPS + rows))

    def inner_body(t, carry):
        march_inner(t)
        return carry

    lax.fori_loop(0, members // TILE, inner_body, 0)
    for side in range(2):

        @pl.when(receives[side])
        def _(side=side):
            forcing_copy(side).wait_recv()
    push(range(1, STEPS))
    push(range(STEPS + rows, rows + 2 * STEPS - 1))

    tiles = per_chunk // TILE
    for c in range(chunks):
        for side in range(2):

            @pl.when(receives[side])
            def _(side=side, c=c):
                for copy in halo_copies(side, c):
                    copy.wait_recv()

        def body(t, carry, c=c):
            march_outer(c * tiles + t)
            return carry

        lax.fori_loop(0, tiles, body, 0, unroll=True)
        for d in range(1, n_mem):
            out_copy(c, d, 0).start()
    for i in range(1, groups):
        for c in range(chunks):
            for d in range(1, n_mem):
                out_copy(c, d, i).start()

    own = pl.ds(pl.multiple_of(me * members, TILE), members)
    for i in range(groups):
        row, col = place(me, i)
        rbuf[i, own, :] = fc[row, :, pl.ds(col, REGION_VALUES)]

    eye = (
        lax.broadcasted_iota(jnp.int32, (obs, obs), 0)
        == lax.broadcasted_iota(jnp.int32, (obs, obs), 1)
    ).astype(f32)
    spread_dof = float(total - 1)

    def prepare(i):
        for c in range(chunks):
            for d in range(1, n_mem):
                out_copy(c, d, i).wait_recv()
        values = rbuf[i]
        mean = jnp.sum(values, axis=0, keepdims=True) * (1.0 / total)
        spread = values - mean
        rbuf[i] = spread
        s_hi, s_lo = split(spread)
        onehot = (
            lax.broadcasted_iota(jnp.int32, (REGION_VALUES, obs), 0) == index_ref[i : i + 1, :]
        ).astype(f32).astype(bf16)
        both = dot(jnp.concatenate([s_hi, s_lo], axis=0), onehot)
        obs_spread = both[:total] + both[total:]
        m_hi = mean.astype(bf16)
        rest = mean - m_hi.astype(f32)
        m_mid = rest.astype(bf16)
        m_lo = (rest - m_mid.astype(f32)).astype(bf16)
        mean_rows = [jnp.broadcast_to(p, (16, REGION_VALUES)) for p in (m_hi, m_mid, m_lo)]
        picked = dot(jnp.concatenate(mean_rows, axis=0), onehot)
        obs_mean = picked[0:1] + picked[16:17] + picked[32:33]
        slots = lax.broadcasted_iota(jnp.int32, (1, obs), 1)
        weight = jnp.where(slots < count_ref[0:1, i : i + 1], prec_ref[i : i + 1, :], 0.0)
        root = jnp.sqrt(weight)
        u_row = root * (value_ref[i : i + 1, :] - obs_mean)
        u_col = jnp.sum(eye * u_row, axis=1, keepdims=True)
        bt = obs_spread * root
        b = bt.T
        bt_wide = wide_lhs(bt)
        bt_ref[i] = bt
        b_hi, b_lo = split(b)
        b_tall = jnp.concatenate([b_hi, b_lo], axis=0)
        k4 = dot(b_tall, bt_wide)
        gram = (k4[:obs, :obs] + k4[obs:, obs:]) + (k4[:obs, obs:] + k4[obs:, :obs])
        e2 = dot(b_tall, s_hi)
        e_ref[i] = e2[:obs] + e2[obs:] + dot(b_hi, s_lo)
        return mean, gram, u_col


    def invert(gram):
        squares = jnp.sum(jnp.sum(gram * gram, axis=0, keepdims=True), axis=1, keepdims=True)
        scale = spread_dof + jnp.sqrt(squares)
        inv = 1.0 / scale
        a0 = spread_dof * inv
        left = a0 * eye + inv * gram
        right = 1.5 * eye - 0.5 * left
        r0 = 1.5 - 0.5 * a0
        l0 = a0 * r0
        rq = None
        rq_scalar = -0.5 * inv
        (left,) = small_dot([left], right)
        for it in range(1, NS_ITERS):
            if rq is None:
                (product,) = small_dot([right], left)
                lq = inv * right + (a0 * rq_scalar) * eye
                pq = rq_scalar * left + r0 * lq
            else:
                product, rq_left = small_dot([right, rq], left)
                lq = inv * right + a0 * rq
                pq = rq_left + r0 * lq
            corr = 1.5 * eye - 0.5 * product
            cq = -0.5 * pq
            c0 = 1.5 - 0.5 * r0 * l0
            last = it == NS_ITERS - 1
            if rq is None:
                rq = rq_scalar * corr + r0 * cq
                left, right = small_dot([left, right], corr)
            elif last:
                right, moved = small_dot([right, rq], corr)
                rq = moved + r0 * cq
            else:
                left, right, moved = small_dot([left, right, rq], corr)
                rq = moved + r0 * cq
            r0, l0 = r0 * c0, l0 * c0
        return scale, right, r0, rq


    def back_copy(d, i):
        peer = lax.rem(me + d, n_mem)
        row, col = place(me, i)
        return pltpu.make_async_remote_copy(
            src_ref=ana.at[i, pl.ds(pl.multiple_of(peer * members, TILE), members), :],
            dst_ref=out_ref.at[row, :, pl.ds(col, REGION_VALUES)],
            send_sem=bsend.at[d - 1, i],
            recv_sem=brecv.at[d - 1, i],
            device_id=(peer, strip),
            device_id_type=MESH,
        )

    for i in range(groups):
        mean, gram, u_col = prepare(i)
        scale, right, r0, rq = invert(gram)
        amp = math.sqrt(spread_dof) / jnp.sqrt(scale)
        e = e_ref[i]
        e_hi, e_lo = split(e)
        rq_wide = wide_lhs(amp * rq)
        z = dot(rq_wide, jnp.concatenate([e_hi, e_hi], axis=0)) + dot(
            rq_wide, jnp.concatenate([e_lo, e_lo], axis=0)
        )
        w1 = jnp.sum(u_col * right, axis=0, keepdims=True)
        w2 = jnp.sum(right * w1, axis=1, keepdims=True) / scale
        shift = mean + jnp.sum(w2 * e, axis=0, keepdims=True)
        z_hi, z_lo = split(z)
        z_high = jnp.concatenate([z_hi, z_hi], axis=0)
        z_low = jnp.concatenate([z_lo, z_lo], axis=0)
        for d in (*range(1, n_mem), 0):
            at = pl.ds(pl.multiple_of(lax.rem(me + d, n_mem) * members, TILE), members)
            bt_wide = wide_lhs(bt_ref[i, at, :])
            moved = dot(bt_wide, z_high) + dot(bt_wide, z_low)
            block = moved + (amp * r0) * rbuf[i, at, :] + shift
            if d:
                ana[i, at, :] = block
                back_copy(d, i).start()
            else:
                row, col = place(me, i)
                out_ref[row, :, pl.ds(col, REGION_VALUES)] = block

    for side in range(2):

        @pl.when(sends[side])
        def _(side=side):
            for copy in all_halo_copies(side):
                copy.wait_send()

    for c in range(chunks):
        for i in range(groups):
            for d in range(1, n_mem):
                out_copy(c, d, i).wait_send()
    for i in range(groups):
        for d in range(1, n_mem):
            back_copy(d, i).wait()


def local(n_mem, n_strip, ensemble, forcing, obs_index, obs_count, obs_value, obs_precision):
    members, rows, lon = ensemble.shape
    groups, obs = obs_index.shape
    total = members * n_mem
    lanes = lon // LANES
    chunks = max(1, members // (2 * TILE))
    vmem = pl.BlockSpec(memory_space=pltpu.VMEM)
    dma = pltpu.SemaphoreType.DMA
    out = pl.pallas_call(
        functools.partial(kernel, n_mem, n_strip, members),
        out_shape=jax.ShapeDtypeStruct((rows, members, lon), f32),
        in_specs=[pl.BlockSpec(memory_space=pl.ANY)] * 6,
        out_specs=vmem,
        scratch_shapes=[
            pltpu.VMEM((1, groups), jnp.int32),
            pltpu.VMEM((groups, obs), jnp.int32),
            pltpu.VMEM((groups, obs), f32),
            pltpu.VMEM((groups, obs), f32),
            pltpu.VMEM((lanes, members, rows, LANES), f32),
            pltpu.VMEM((lanes, members, rows, LANES), f32),
            pltpu.VMEM((3, rows, lon), f32),
            pltpu.VMEM((rows + 2 * STEPS, TILE, lon), f32),
            pltpu.VMEM((STEPS * rows, members, lon), f32),
            pltpu.VMEM((rows, members, lon), f32),
            pltpu.VMEM((groups, total, REGION_VALUES), f32),
            pltpu.VMEM((groups, total, REGION_VALUES), f32),
            pltpu.VMEM((groups, total, obs), f32),
            pltpu.VMEM((groups, obs, REGION_VALUES), f32),
            dma((2, chunks, lanes)),
            dma((2, chunks, lanes)),
            dma((chunks, n_mem - 1, groups)),
            dma((chunks, n_mem - 1, groups)),
            dma((n_mem - 1, groups)),
            dma((n_mem - 1, groups)),
            dma((2,)),
            dma((2,)),
            dma((lanes + 5,)),
        ],
        compiler_params=pltpu.CompilerParams(
            collective_id=0, has_side_effects=True, vmem_limit_bytes=48 * 1024 * 1024
        ),
    )(*[pltpu.with_memory_space_constraint(a, pltpu.HBM) for a in (ensemble, forcing, obs_index, obs_count[None], obs_value, obs_precision)])
    return jnp.transpose(out, (1, 0, 2))


def solution(mesh):
    placed = (
        P("mem", "strip", None),
        P("strip", None),
        P(("strip", "mem"), None),
        P(("strip", "mem")),
        P(("strip", "mem"), None),
        P(("strip", "mem"), None),
    )
    return jax.shard_map(
        functools.partial(local, mesh.shape["mem"], mesh.shape["strip"]),
        mesh=mesh,
        in_specs=placed,
        out_specs=P("mem", "strip", None),
        check_vma=False,
    )
```
